32 devices in a mesh: grp: 2 (over core), brick: 16 (over z, y, x).
Axes of the slice: x: 2, y: 2, z: 4, core: 2. Of those that a mesh axis runs over, the one named last changes fastest.
Arguments:
- density: float32 [64, 64, 256], P('brick', None, 'grp'), may hold values from 0.5 to 2
- energy_field: float32 [64, 64, 256], P('brick', None, 'grp'), may hold values from -6 to 6
- lepton_field: float32 [64, 64, 256], P('brick', None, 'grp'), may hold values from 0.1 to 0.6
- velocity: float32 [3, 64, 64, 256], P(None, 'brick', None, 'grp'), may hold values from -4 to 4
- abundance: float32 [2, 16, 1024, 128], P('grp', 'brick'), may hold values from -1.2 to 1.2
- tracer_mass: float32 [2, 16, 1024], P('grp', 'brick'), may hold values from 0.2 to 1
- tracer_cell: int32 [2, 16, 1024], P('grp', 'brick'), may hold values from 0 to 32767
- tracer_count: int32 [2, 16], P('grp', 'brick'), may hold values from 1 to 1024, as said below
- weak_rates: float32 [128, 128], replicated, may hold values from -0.5 to 0.5
- capture_rates: float32 [128, 128], replicated, may hold values from -0.5 to 0.5
- binding: float32 [128], replicated, may hold values from -6 to 6
- charge_ratio: float32 [128], replicated, may hold values from 0 to 1
Outputs:
- density_out: float32 [64, 64, 256], P('brick', None, 'grp')
- energy_out: float32 [64, 64, 256], P('brick', None, 'grp')
- lepton_out: float32 [64, 64, 256], P('brick', None, 'grp')
- abundance_out: float32 [2, 16, 1024, 128], P('grp', 'brick')
The draws below stay inside these ranges and needn't reach their ends.
Inputs may be any that keep to these rules, and one draw needn't show every extreme that they name: `tracer_count`: for each index of grp the counts sum to 8192; exactly one brick of each half holds 1024, the most; every other brick holds at most 512, and some brick of each half holds exactly 512.
All inputs are finite; a program needn't handle non-finite values.
Results may differ from the reference program's by a relative error of at most 0.00029.
Values sent between devices are 32-bit elements; how exact they have to be, the bound alone decides.
A program may use at most 64 MiB of HBM per device.

```python
import math
import jax
import jax.numpy as jnp
from jax import lax

S = 128
CX = 4
CY = 64
CZ = 128
TR_DEV = 512
NEWTON = 2
SWEEPS = 8
TCAP = 1024
NX = 64
NZ = 256
N_GRP = 2
N_BRICK = 16


def draw_tracer_count(key, part):
    first_key, second_key, third_key = jax.random.split(key, 3)
    busiest = jax.random.randint(first_key, (N_GRP,), 0, N_BRICK)
    offset = jax.random.randint(third_key, (N_GRP,), 1, N_BRICK)
    filled = (busiest + offset) % N_BRICK
    weights = jax.random.randint(second_key, (N_GRP, N_BRICK), 1, 4)
    brick_ids = jnp.arange(N_BRICK, dtype=jnp.int32)[None, :]
    is_busiest = brick_ids == busiest[:, None]
    is_filled = brick_ids == filled[:, None]
    others = jnp.logical_not(jnp.logical_or(is_busiest, is_filled)).astype(jnp.int32)
    weights = weights * others
    shares = weights * TR_DEV // jnp.sum(weights, axis=1, keepdims=True)
    leftover = TR_DEV - jnp.sum(shares, axis=1, keepdims=True)
    rank_order = jnp.cumsum(others, axis=1) - 1
    shares = shares + others * (rank_order < leftover).astype(jnp.int32)
    return jnp.where(is_busiest, TCAP, TR_DEV - shares).astype(jnp.int32)


def with_ends(array, stream_key, smallest, top_value):
    shape = array.shape
    place = [jax.random.randint(jax.random.fold_in(stream_key, axis), (), 0, shape[axis]) for axis in range(len(shape))]
    array = array.at[tuple(place)].set(smallest)
    longest = shape.index(max(shape))
    place[longest] = (place[longest] + 1) % shape[longest]
    return array.at[tuple(place)].set(top_value)


def block_scale(own_key, shape, pieces, smallest, high):
    loudness = 1.0
    for axis_at, shards_of in pieces:
        heights = jax.random.uniform(jax.random.fold_in(jax.random.fold_in(own_key, 6), axis_at), (shards_of,), jnp.float32, smallest / len(pieces), high / len(pieces))
        loudness = loudness * jnp.repeat(jnp.exp(heights), shape[axis_at] // shards_of).reshape((-1,) + (1,) * (len(shape) - 1 - axis_at))
    return loudness


def centred(stream_key, extent, deviation, bound, cuts=(), kind=jnp.bfloat16):
    values = deviation * jax.random.normal(stream_key, extent, jnp.float32)
    if cuts:
        values = values * block_scale(stream_key, extent, cuts, -0.22, 0.18)
    return jnp.clip(values, -bound, bound).astype(kind)


def setup_inputs(seed: int = 0) -> dict:
    keys = jax.random.split(jax.random.key(seed), 13)
    return {
        "density": jnp.clip(jnp.exp(math.log(2.0) - 1.3862944 * jax.random.uniform(keys[0], (NX, CY, NZ), jnp.float32) ** block_scale(keys[0], (NX, CY, NZ), ((0, 16), (2, 2)), -0.2, 0.2)), 0.5, 2.0),
        "energy_field": centred(keys[1], (NX, CY, NZ), 1.0, 6.0, ((0, 16), (2, 2)), jnp.float32),
        "lepton_field": jnp.clip(0.1 + 0.5 * jax.random.uniform(keys[2], (NX, CY, NZ), jnp.float32) ** block_scale(keys[2], (NX, CY, NZ), ((0, 16), (2, 2)), -0.2, 0.2), 0.1, 0.6),
        "velocity": centred(keys[3], (3, NX, CY, NZ), 1.0, 4.0, ((1, 16), (3, 2)), jnp.float32),
        "abundance": centred(keys[4], (N_GRP, N_BRICK, TCAP, S), 0.3, 1.2, ((0, 2), (1, 16)), jnp.float32),
        "tracer_mass": jnp.clip(jnp.exp(math.log(1.0) - 1.609438 * jax.random.uniform(keys[5], (N_GRP, N_BRICK, TCAP), jnp.float32) ** block_scale(keys[5], (N_GRP, N_BRICK, TCAP), ((0, 2), (1, 16)), -0.2, 0.2)), 0.2, 1.0),
        "tracer_cell": with_ends(jax.random.randint(keys[6], (N_GRP, N_BRICK, TCAP), 0, CX * CY * CZ), jax.random.fold_in(keys[6], 1), 0, (CX * CY * CZ) - 1).astype(jnp.int32),
        "tracer_count": draw_tracer_count(jax.random.fold_in(keys[12], 71), 0),
        "weak_rates": centred(keys[8], (S, S), S ** -0.5, 0.5, (), jnp.float32),
        "capture_rates": centred(keys[9], (S, S), S ** -0.5, 0.5, (), jnp.float32),
        "binding": centred(keys[10], (S,), 1.0, 6.0, (), jnp.float32),
        "charge_ratio": jnp.clip(jax.random.uniform(keys[11], (S,), jnp.float32, 0.0, 1.0), 0.0, 1.0),
    }


courant = 0.8
highest = lax.Precision.HIGHEST


def rolled_difference(values, axis_number):
    return (8.0 * (jnp.roll(values, -1, axis_number) - jnp.roll(values, 1, axis_number)) - (jnp.roll(values, -2, axis_number) - jnp.roll(values, 2, axis_number))) / 12.0


def full_tendency(fields, speeds):
    along_x = rolled_difference(speeds[0][None] * fields, 1)
    along_y = rolled_difference(speeds[1][None] * fields, 2)
    along_z = rolled_difference(speeds[2][None] * fields, 3)
    return -((along_x + along_y) + along_z)


def thermo_rates(density, energy_field, lepton_field, cells):
    thermo = jnp.stack([density, energy_field, lepton_field]).reshape(3, -1)
    picked = jnp.take(thermo, cells, axis=1)
    weak_scale = 0.62 + 0.04 * picked[0] + 0.05 * (picked[2] / picked[0])
    capture_scale = 0.3 * jax.nn.sigmoid(picked[1] / picked[0])
    return weak_scale, capture_scale


def network_step(initial, rate_weak, rate_capture, matrices):
    species = initial.shape[1]
    iterate = initial
    for newton_turn in range(NEWTON):
        products = jnp.dot(iterate, matrices, precision=highest, preferred_element_type=jnp.float32)
        alpha_part = iterate[:, 0:1]
        capture = products[:, species:]
        target = -(iterate - initial - (rate_weak * products[:, :species] + rate_capture * alpha_part * capture))
        update = target
        for sweep_turn in range(SWEEPS):
            product = jnp.dot(update, matrices, precision=highest, preferred_element_type=jnp.float32)
            update = target + (rate_weak * product[:, :species] + rate_capture * alpha_part * product[:, species:] + rate_capture * update[:, 0:1] * capture)
        iterate = iterate + update
    return iterate


def reference(density, energy_field, lepton_field, velocity, abundance, tracer_mass, tracer_cell, tracer_count, weak_rates, capture_rates, binding, charge_ratio):
    state = jnp.stack([density, energy_field, lepton_field])
    midpoint = state + (0.5 * courant) * full_tendency(state, velocity)
    advanced = state + courant * full_tendency(midpoint, velocity)
    groups_z, groups_x, capacity = tracer_cell.shape
    plane = CY * CZ
    cell_x = tracer_cell // plane
    cell_y = (tracer_cell // CZ) % CY
    cell_z = tracer_cell % CZ
    grp_ids = jnp.arange(groups_z, dtype=jnp.int32)[:, None, None]
    brick_ids = jnp.arange(groups_x, dtype=jnp.int32)[None, :, None]
    global_cell = ((brick_ids * CX + cell_x) * CY + cell_y) * NZ + grp_ids * CZ + cell_z
    flat_ids = global_cell.reshape(-1).astype(jnp.int32)
    weak_scale, capture_scale = thermo_rates(density, energy_field, lepton_field, flat_ids)
    occupied = (jnp.arange(capacity, dtype=jnp.int32)[None, None, :] < tracer_count[:, :, None]).reshape(-1, capacity)
    rows = abundance.reshape(-1, capacity, S)
    rates = jnp.stack([weak_scale, capture_scale], axis=1).reshape(-1, capacity, 2)
    matrices = jnp.concatenate([weak_rates, capture_rates], axis=1)

    def solve_block(block_item):
        return network_step(block_item[0], block_item[1][:, 0:1], block_item[1][:, 1:2], matrices)

    solved = lax.map(solve_block, (rows, rates))
    finished = jnp.where(occupied[..., None], solved, 0.0)
    initial = jnp.where(occupied[..., None], rows, 0.0)
    change = (finished - initial).reshape(-1, S)
    table = jnp.stack([binding, charge_ratio], axis=1)
    gains = jnp.dot(change, table, precision=highest, preferred_element_type=jnp.float32) * tracer_mass.reshape(-1)[:, None]
    deposit = jnp.zeros((NX * CY * NZ, 2), jnp.float32).at[flat_ids].add(gains)
    energy_out = advanced[1] + deposit[:, 0].reshape(NX, CY, NZ)
    lepton_out = advanced[2] + deposit[:, 1].reshape(NX, CY, NZ)
    return advanced[0], energy_out, lepton_out, finished.reshape(abundance.shape)
```

```python
import functools

import jax
import jax.numpy as jnp
from jax import lax
from jax.experimental import pallas as pl
from jax.experimental.pallas import tpu as pltpu
from jax.sharding import PartitionSpec as P

NEWTON = 2
SWEEPS = 8
courant = 0.8
f32 = jnp.float32
bf16 = jnp.bfloat16
BLOCK = 256
MESH = pl.DeviceIdType.MESH


def split(values):
    high = values.astype(bf16)
    low = (values - high.astype(f32)).astype(bf16)
    return high, low


def dot(a, b, dims=((1,), (0,))):
    return lax.dot_general(a, b, (dims, ((), ())), preferred_element_type=f32)


def five_point(lower2, lower1, upper1, upper2):
    return 8.0 * (upper1 - lower1) - (upper2 - lower2)


def y_part(g):
    n = g.shape[0]
    return five_point(
        pltpu.roll(g, 2, 0), pltpu.roll(g, 1, 0), pltpu.roll(g, n - 1, 0), pltpu.roll(g, n - 2, 0)
    )


def z_part(h, other):
    n = h.shape[1]
    lane = lax.broadcasted_iota(jnp.int32, h.shape, 1)
    return five_point(
        pltpu.roll(jnp.where(lane >= n - 2, other, h), 2, 1),
        pltpu.roll(jnp.where(lane >= n - 1, other, h), 1, 1),
        pltpu.roll(jnp.where(lane < 1, other, h), n - 1, 1),
        pltpu.roll(jnp.where(lane < 2, other, h), n - 2, 1),
    )


def kernel(
    axis_sizes,
    count_ref,
    rho_ref,
    eps_ref,
    lam_ref,
    vel_ref,
    rows_ref,
    mass_ref,
    cell_ref,
    weak_ref,
    capture_ref,
    table_ref,
    density_out,
    energy_out,
    lepton_out,
    abundance_out,
    xs,
    zs,
    low_in,
    high_in,
    z_in,
    mid,
    weights,
    onehot,
    rate_weak,
    rate_capture,
    start_rows,
    alpha_capture,
    scaled_capture,
    target,
    update,
    deposit,
    send_sem,
    recv_sem,
):
    n_grp, n_brick = axis_sizes
    g = lax.axis_index("grp")
    b = lax.axis_index("brick")
    right = (g, lax.rem(b + 1, n_brick))
    left = (g, lax.rem(b + n_brick - 1, n_brick))
    partner = (lax.rem(g + 1, n_grp), b)
    fields = (rho_ref, eps_ref, lam_ref)
    outs = (density_out, energy_out, lepton_out)
    cx, cy, cz = rho_ref.shape
    capacity, species = rows_ref.shape

    barrier = pltpu.get_barrier_semaphore()
    for neighbour in (left, right, partner):
        pl.semaphore_signal(barrier, inc=1, device_id=neighbour, device_id_type=MESH)

    for f in range(3):
        for p in range(cx):
            xs[0, f, p] = vel_ref[0, p] * fields[f][p]
            zs[0, f, p] = vel_ref[2, p] * fields[f][p]

    pl.semaphore_wait(barrier, 3)

    def copies(stage, f):
        made = []
        for k, (src, dst, device) in enumerate(
            (
                (xs.at[stage, f, pl.ds(0, 2)], high_in.at[stage, f], left),
                (xs.at[stage, f, pl.ds(cx - 2, 2)], low_in.at[stage, f], right),
                (zs.at[stage, f], z_in.at[stage, f], partner),
            )
        ):
            made.append(
                pltpu.make_async_remote_copy(
                    src_ref=src,
                    dst_ref=dst,
                    send_sem=send_sem.at[stage, f, k],
                    recv_sem=recv_sem.at[stage, f, k],
                    device_id=device,
                    device_id_type=MESH,
                )
            )
        return made

    started = [[copies(stage, f) for f in range(3)] for stage in range(2)]
    for f in range(3):
        for copy in started[0][f]:
            copy.start()

    cells = cell_ref[...]
    cell_row = cells // cz
    cell_lane = cells - cell_row * cz
    row_ids = lax.broadcasted_iota(jnp.int32, (cx * cy, capacity), 0)
    onehot[...] = jnp.where(row_ids == cell_row, 1.0, 0.0).astype(bf16)
    lane_ids = lax.broadcasted_iota(jnp.int32, (cz, capacity), 0)
    lane_hit = lane_ids == cell_lane
    picked = []
    for f in range(3):
        high, low = split(fields[f][...].reshape(cx * cy, cz))
        found = dot(high, onehot[...], ((0,), (0,))) + dot(low, onehot[...], ((0,), (0,)))
        picked.append(jnp.sum(jnp.where(lane_hit, found, 0.0), axis=0, keepdims=True))
    rho, eps, lam = picked
    weak_row = 0.62 + 0.04 * rho + 0.05 * (lam / rho)
    capture_row = 0.3 * jax.nn.sigmoid(eps / rho)
    for k in range(capacity // 128):
        part = pl.ds(k * 128, 128)
        cols = slice(k * 128, k * 128 + 128)
        rate_weak[part, :] = jnp.broadcast_to(weak_row[:, cols], (128, 128)).T
        rate_capture[part, :] = jnp.broadcast_to(capture_row[:, cols], (128, 128)).T

    for k, ref in enumerate((weak_ref, capture_ref)):
        high, low = split(ref[...])
        cols = pl.ds(k * species, species)
        weights[0:species, cols] = high
        weights[species : 2 * species, cols] = high
        weights[2 * species : 3 * species, cols] = low

    count = count_ref[0, 0]
    for k in range(capacity // BLOCK):
        part = pl.ds(k * BLOCK, BLOCK)
        row = lax.broadcasted_iota(jnp.int32, (BLOCK, species), 0) + k * BLOCK
        first = jnp.where(row < count, rows_ref[part, :], 0.0)
        start_rows[part, :] = first
        abundance_out[part, :] = first

    def product(values):
        high, low = split(values)
        return dot(jnp.concatenate([high, low, high], axis=1), weights[...])

    def newton(turn):
        for k in range(capacity // BLOCK):
            part = pl.ds(k * BLOCK, BLOCK)
            now = abundance_out[part, :]
            made = product(now)
            capture = made[:, species:]
            scaled = rate_capture[part, :]
            alpha = scaled * now[:, 0:1]
            alpha_capture[part, :] = alpha
            scaled_capture[part, :] = scaled * capture
            aim = rate_weak[part, :] * made[:, :species] + alpha * capture
            if turn:
                aim = aim - (now - start_rows[part, :])
            target[part, :] = aim
            update[part, :] = aim

        def sweep(_, carry):
            for k in range(capacity // BLOCK):
                part = pl.ds(k * BLOCK, BLOCK)
                now = update[part, :]
                made = product(now)
                update[part, :] = target[part, :] + (
                    rate_weak[part, :] * made[:, :species]
                    + alpha_capture[part, :] * made[:, species:]
                    + scaled_capture[part, :] * now[:, 0:1]
                )
            return carry

        lax.fori_loop(0, SWEEPS, sweep, 0)
        for k in range(capacity // BLOCK):
            part = pl.ds(k * BLOCK, BLOCK)
            abundance_out[part, :] = abundance_out[part, :] + update[part, :]

    def tendency(stage, f, field):
        results = []
        line = (
            [low_in[stage, f, 0], low_in[stage, f, 1]]
            + [xs[stage, f, p] for p in range(cx)]
            + [high_in[stage, f, 0], high_in[stage, f, 1]]
        )
        for p in range(cx):
            along_x = five_point(line[p], line[p + 1], line[p + 3], line[p + 4])
            along_y = y_part(vel_ref[1, p] * field[p])
            along_z = z_part(zs[stage, f, p], z_in[stage, f, p])
            results.append((along_x + along_y + along_z) * (-1.0 / 12.0))
        return results

    newton(0)

    for f in range(3):
        for copy in started[0][f]:
            copy.wait_recv()
        slopes = tendency(0, f, [fields[f][p] for p in range(cx)])
        for p in range(cx):
            half = fields[f][p] + 0.5 * courant * slopes[p]
            mid[f, p] = half
            xs[1, f, p] = vel_ref[0, p] * half
            zs[1, f, p] = vel_ref[2, p] * half
        for copy in started[1][f]:
            copy.start()

    newton(1)

    change_high, change_low = split(abundance_out[...] - start_rows[...])
    table_high, table_low = split(table_ref[...])
    gains = (
        dot(table_high, change_high, ((1,), (1,)))
        + dot(table_high, change_low, ((1,), (1,)))
        + dot(table_low, change_high, ((1,), (1,)))
    ) * mass_ref[...]
    for k in range(2):
        placed = jnp.where(lane_hit, gains[k : k + 1, :], 0.0)
        high, low = split(placed)
        deposit[k] = (
            dot(onehot[...], high, ((1,), (1,))) + dot(onehot[...], low, ((1,), (1,)))
        ).reshape(cx, cy, cz)

    for f in range(3):
        for copy in started[1][f]:
            copy.wait_recv()
        slopes = tendency(1, f, [mid[f, p] for p in range(cx)])
        for p in range(cx):
            value = fields[f][p] + courant * slopes[p]
            if f:
                value = value + deposit[f - 1, p]
            outs[f][p] = value

    for stage in range(2):
        for f in range(3):
            for copy in started[stage][f]:
                copy.wait_send()


def on_device(
    axis_sizes,
    density,
    energy_field,
    lepton_field,
    velocity,
    abundance,
    tracer_mass,
    tracer_cell,
    tracer_count,
    weak_rates,
    capture_rates,
    binding,
    charge_ratio,
):
    cx, cy, cz = density.shape
    capacity, species = abundance.shape[2:]
    table = jnp.zeros((8, species), f32).at[0].set(binding).at[1].set(charge_ratio)
    vmem = pl.BlockSpec(memory_space=pltpu.VMEM)
    field = jax.ShapeDtypeStruct(density.shape, f32)
    rows = pltpu.VMEM((capacity, species), f32)
    advanced = pl.pallas_call(
        functools.partial(kernel, axis_sizes),
        out_shape=(field, field, field, jax.ShapeDtypeStruct((capacity, species), f32)),
        in_specs=[pl.BlockSpec(memory_space=pltpu.SMEM)] + [vmem] * 10,
        out_specs=(vmem,) * 4,
        scratch_shapes=[
            pltpu.VMEM((2, 3, cx, cy, cz), f32),
            pltpu.VMEM((2, 3, cx, cy, cz), f32),
            pltpu.VMEM((2, 3, 2, cy, cz), f32),
            pltpu.VMEM((2, 3, 2, cy, cz), f32),
            pltpu.VMEM((2, 3, cx, cy, cz), f32),
            pltpu.VMEM((3, cx, cy, cz), f32),
            pltpu.VMEM((3 * species, 2 * species), bf16),
            pltpu.VMEM((cx * cy, capacity), bf16),
            rows,
            rows,
            rows,
            rows,
            rows,
            rows,
            rows,
            pltpu.VMEM((2, cx, cy, cz), f32),
            pltpu.SemaphoreType.DMA((2, 3, 3)),
            pltpu.SemaphoreType.DMA((2, 3, 3)),
        ],
        compiler_params=pltpu.CompilerParams(collective_id=0, has_side_effects=True),
    )(
        tracer_count,
        density,
        energy_field,
        lepton_field,
        velocity,
        abundance.reshape(capacity, species),
        tracer_mass.reshape(1, capacity),
        tracer_cell.reshape(1, capacity),
        weak_rates,
        capture_rates,
        table,
    )
    return advanced[0], advanced[1], advanced[2], advanced[3][None, None]


def solution(mesh):
    sizes = (mesh.shape["grp"], mesh.shape["brick"])
    assert sizes[0] == 2
    return jax.shard_map(
        functools.partial(on_device, sizes),
        mesh=mesh,
        in_specs=(
            P("brick", None, "grp"),
            P("brick", None, "grp"),
            P("brick", None, "grp"),
            P(None, "brick", None, "grp"),
            P("grp", "brick", None, None),
            P("grp", "brick", None),
            P("grp", "brick", None),
            P("grp", "brick"),
            P(),
            P(),
            P(),
            P(),
        ),
        out_specs=(
            P("brick", None, "grp"),
            P("brick", None, "grp"),
            P("brick", None, "grp"),
            P("grp", "brick", None, None),
        ),
        check_vma=False,
    )
```

```python
import functools

import jax
import jax.numpy as jnp
from jax import lax
from jax.experimental import pallas as pl
from jax.experimental.pallas import tpu as pltpu
from jax.sharding import PartitionSpec as P

NEWTON = 2
SWEEPS = 8
courant = 0.8
f32 = jnp.float32
bf16 = jnp.bfloat16
BLOCK = 256
MESH = pl.DeviceIdType.MESH


def split(values):
    high = values.astype(bf16)
    low = (values - high.astype(f32)).astype(bf16)
    return high, low


def dot(a, b, dims=((1,), (0,))):
    return lax.dot_general(a, b, (dims, ((), ())), preferred_element_type=f32)


def five_point(lower2, lower1, upper1, upper2):
    return 8.0 * (upper1 - lower1) - (upper2 - lower2)


def y_part(g):
    n = g.shape[0]
    return five_point(
        pltpu.roll(g, 2, 0), pltpu.roll(g, 1, 0), pltpu.roll(g, n - 1, 0), pltpu.roll(g, n - 2, 0)
    )


def z_part(h, other):
    n = h.shape[1]
    lane = lax.broadcasted_iota(jnp.int32, h.shape, 1)
    return five_point(
        pltpu.roll(jnp.where(lane >= n - 2, other, h), 2, 1),
        pltpu.roll(jnp.where(lane >= n - 1, other, h), 1, 1),
        pltpu.roll(jnp.where(lane < 1, other, h), n - 1, 1),
        pltpu.roll(jnp.where(lane < 2, other, h), n - 2, 1),
    )


def kernel(
    axis_sizes,
    count_ref,
    rho_ref,
    eps_ref,
    lam_ref,
    vel_ref,
    rows_ref,
    mass_ref,
    cell_ref,
    weak_ref,
    capture_ref,
    binding_ref,
    charge_ref,
    density_out,
    energy_out,
    lepton_out,
    abundance_out,
    xs,
    zs,
    low_in,
    high_in,
    z_in,
    mid,
    weights,
    onehot,
    rate_weak,
    rate_capture,
    start_rows,
    alpha_capture,
    scaled_capture,
    target,
    update,
    deposit,
    send_sem,
    recv_sem,
):
    n_grp, n_brick = axis_sizes
    g = lax.axis_index("grp")
    b = lax.axis_index("brick")
    right = (g, lax.rem(b + 1, n_brick))
    left = (g, lax.rem(b + n_brick - 1, n_brick))
    partner = (lax.rem(g + 1, n_grp), b)
    fields = (rho_ref, eps_ref, lam_ref)
    outs = (density_out, energy_out, lepton_out)
    cx, cy, cz = rho_ref.shape
    capacity, species = rows_ref.shape

    barrier = pltpu.get_barrier_semaphore()
    for neighbour in (left, right, partner):
        pl.semaphore_signal(barrier, inc=1, device_id=neighbour, device_id_type=MESH)

    for f in range(3):
        for p in range(cx):
            xs[0, f, p] = vel_ref[0, p] * fields[f][p]
            zs[0, f, p] = vel_ref[2, p] * fields[f][p]

    pl.semaphore_wait(barrier, 3)

    def copies(stage, f):
        made = []
        for k, (src, dst, device) in enumerate(
            (
                (xs.at[stage, f, pl.ds(0, 2)], high_in.at[stage, f], left),
                (xs.at[stage, f, pl.ds(cx - 2, 2)], low_in.at[stage, f], right),
                (zs.at[stage, f], z_in.at[stage, f], partner),
            )
        ):
            made.append(
                pltpu.make_async_remote_copy(
                    src_ref=src,
                    dst_ref=dst,
                    send_sem=send_sem.at[stage, f, k],
                    recv_sem=recv_sem.at[stage, f, k],
                    device_id=device,
                    device_id_type=MESH,
                )
            )
        return made

    started = [[copies(stage, f) for f in range(3)] for stage in range(2)]
    for f in range(3):
        for copy in started[0][f]:
            copy.start()

    cells = cell_ref[...]
    cell_row = cells // cz
    cell_lane = cells - cell_row * cz
    row_ids = lax.broadcasted_iota(jnp.int32, (cx * cy, capacity), 0)
    onehot[...] = jnp.where(row_ids == cell_row, 1.0, 0.0).astype(bf16)
    lane_ids = lax.broadcasted_iota(jnp.int32, (cz, capacity), 0)
    lane_hit = lane_ids == cell_lane
    picked = []
    for f in range(3):
        high, low = split(fields[f][...].reshape(cx * cy, cz))
        found = dot(high, onehot[...], ((0,), (0,))) + dot(low, onehot[...], ((0,), (0,)))
        picked.append(jnp.sum(jnp.where(lane_hit, found, 0.0), axis=0, keepdims=True))
    rho, eps, lam = picked
    weak_row = 0.62 + 0.04 * rho + 0.05 * (lam / rho)
    capture_row = 0.3 * jax.nn.sigmoid(eps / rho)
    for k in range(capacity // 128):
        part = pl.ds(k * 128, 128)
        cols = slice(k * 128, k * 128 + 128)
        rate_weak[part, :] = jnp.broadcast_to(weak_row[:, cols], (128, 128)).T
        rate_capture[part, :] = jnp.broadcast_to(capture_row[:, cols], (128, 128)).T

    for k, ref in enumerate((weak_ref, capture_ref)):
        high, low = split(ref[...])
        cols = pl.ds(k * species, species)
        weights[0:species, cols] = high
        weights[species : 2 * species, cols] = high
        weights[2 * species : 3 * species, cols] = low

    count = count_ref[0, 0]
    for k in range(capacity // BLOCK):
        part = pl.ds(k * BLOCK, BLOCK)
        row = lax.broadcasted_iota(jnp.int32, (BLOCK, species), 0) + k * BLOCK
        first = jnp.where(row < count, rows_ref[part, :], 0.0)
        start_rows[part, :] = first
        abundance_out[part, :] = first

    def product(values):
        high, low = split(values)
        return dot(jnp.concatenate([high, low, high], axis=1), weights[...])

    def newton(turn):
        for k in range(capacity // BLOCK):
            part = pl.ds(k * BLOCK, BLOCK)
            now = abundance_out[part, :]
            made = product(now)
            capture = made[:, species:]
            scaled = rate_capture[part, :]
            alpha = scaled * now[:, 0:1]
            alpha_capture[part, :] = alpha
            scaled_capture[part, :] = scaled * capture
            aim = rate_weak[part, :] * made[:, :species] + alpha * capture
            if turn:
                aim = aim - (now - start_rows[part, :])
            target[part, :] = aim
            update[part, :] = aim

        def sweep(_, carry):
            for k in range(capacity // BLOCK):
                part = pl.ds(k * BLOCK, BLOCK)
                now = update[part, :]
                made = product(now)
                update[part, :] = target[part, :] + (
                    rate_weak[part, :] * made[:, :species]
                    + alpha_capture[part, :] * made[:, species:]
                    + scaled_capture[part, :] * now[:, 0:1]
                )
            return carry

        lax.fori_loop(0, SWEEPS, sweep, 0)
        for k in range(capacity // BLOCK):
            part = pl.ds(k * BLOCK, BLOCK)
            abundance_out[part, :] = abundance_out[part, :] + update[part, :]

    def tendency(stage, f, field):
        results = []
        line = (
            [low_in[stage, f, 0], low_in[stage, f, 1]]
            + [xs[stage, f, p] for p in range(cx)]
            + [high_in[stage, f, 0], high_in[stage, f, 1]]
        )
        for p in range(cx):
            along_x = five_point(line[p], line[p + 1], line[p + 3], line[p + 4])
            along_y = y_part(vel_ref[1, p] * field[p])
            along_z = z_part(zs[stage, f, p], z_in[stage, f, p])
            results.append((along_x + along_y + along_z) * (-1.0 / 12.0))
        return results

    newton(0)

    for f in range(3):
        for copy in started[0][f]:
            copy.wait_recv()
        slopes = tendency(0, f, [fields[f][p] for p in range(cx)])
        for p in range(cx):
            half = fields[f][p] + 0.5 * courant * slopes[p]
            mid[f, p] = half
            xs[1, f, p] = vel_ref[0, p] * half
            zs[1, f, p] = vel_ref[2, p] * half
        for copy in started[1][f]:
            copy.start()

    newton(1)

    change_high, change_low = split(abundance_out[...] - start_rows[...])
    table = jnp.concatenate(
        [binding_ref[...], charge_ref[...], jnp.zeros((6, species), f32)], axis=0
    )
    table_high, table_low = split(table)
    gains = (
        dot(table_high, change_high, ((1,), (1,)))
        + dot(table_high, change_low, ((1,), (1,)))
        + dot(table_low, change_high, ((1,), (1,)))
    ) * mass_ref[...]
    for k in range(2):
        placed = jnp.where(lane_hit, gains[k : k + 1, :], 0.0)
        high, low = split(placed)
        deposit[k] = (
            dot(onehot[...], high, ((1,), (1,))) + dot(onehot[...], low, ((1,), (1,)))
        ).reshape(cx, cy, cz)

    for f in range(3):
        for copy in started[1][f]:
            copy.wait_recv()
        slopes = tendency(1, f, [mid[f, p] for p in range(cx)])
        for p in range(cx):
            value = fields[f][p] + courant * slopes[p]
            if f:
                value = value + deposit[f - 1, p]
            outs[f][p] = value

    for stage in range(2):
        for f in range(3):
            for copy in started[stage][f]:
                copy.wait_send()


def settle(a_ref, b_ref, c_ref, d_ref, a_out, b_out, c_out, d_out, sem):
    pairs = ((d_ref, d_out), (a_ref, a_out), (b_ref, b_out), (c_ref, c_out))
    moves = [pltpu.make_async_copy(src, dst, sem.at[k]) for k, (src, dst) in enumerate(pairs)]
    for move in moves:
        move.start()
    for move in moves:
        move.wait()


def on_device(
    axis_sizes,
    density,
    energy_field,
    lepton_field,
    velocity,
    abundance,
    tracer_mass,
    tracer_cell,
    tracer_count,
    weak_rates,
    capture_rates,
    binding,
    charge_ratio,
):
    cx, cy, cz = density.shape
    capacity, species = abundance.shape[2:]
    vmem = pl.BlockSpec(memory_space=pltpu.VMEM)
    field = jax.ShapeDtypeStruct(density.shape, f32)
    rows = pltpu.VMEM((capacity, species), f32)
    advanced = pl.pallas_call(
        functools.partial(kernel, axis_sizes),
        out_shape=(pltpu.VMEM(density.shape, f32),) * 3 + (rows,),
        in_specs=[pl.BlockSpec(memory_space=pltpu.SMEM)] + [vmem] * 11,
        out_specs=(vmem,) * 4,
        scratch_shapes=[
            pltpu.VMEM((2, 3, cx, cy, cz), f32),
            pltpu.VMEM((2, 3, cx, cy, cz), f32),
            pltpu.VMEM((2, 3, 2, cy, cz), f32),
            pltpu.VMEM((2, 3, 2, cy, cz), f32),
            pltpu.VMEM((2, 3, cx, cy, cz), f32),
            pltpu.VMEM((3, cx, cy, cz), f32),
            pltpu.VMEM((3 * species, 2 * species), bf16),
            pltpu.VMEM((cx * cy, capacity), bf16),
            rows,
            rows,
            rows,
            rows,
            rows,
            rows,
            rows,
            pltpu.VMEM((2, cx, cy, cz), f32),
            pltpu.SemaphoreType.DMA((2, 3, 3)),
            pltpu.SemaphoreType.DMA((2, 3, 3)),
        ],
        compiler_params=pltpu.CompilerParams(collective_id=0, has_side_effects=True),
    )(
        tracer_count,
        density,
        energy_field,
        lepton_field,
        velocity,
        abundance.reshape(capacity, species),
        tracer_mass.reshape(1, capacity),
        tracer_cell.reshape(1, capacity),
        weak_rates,
        capture_rates,
        binding.reshape(1, species),
        charge_ratio.reshape(1, species),
    )
    whole = pl.BlockSpec(memory_space=pl.ANY)
    results = pl.pallas_call(
        settle,
        out_shape=(field, field, field, jax.ShapeDtypeStruct((capacity, species), f32)),
        in_specs=[whole] * 4,
        out_specs=(whole,) * 4,
        scratch_shapes=[pltpu.SemaphoreType.DMA((4,))],
    )(*[pltpu.with_memory_space_constraint(a, pltpu.VMEM) for a in advanced])
    return results[0], results[1], results[2], results[3][None, None]


def solution(mesh):
    sizes = (mesh.shape["grp"], mesh.shape["brick"])
    assert sizes[0] == 2
    return jax.shard_map(
        functools.partial(on_device, sizes),
        mesh=mesh,
        in_specs=(
            P("brick", None, "grp"),
            P("brick", None, "grp"),
            P("brick", None, "grp"),
            P(None, "brick", None, "grp"),
            P("grp", "brick", None, None),
            P("grp", "brick", None),
            P("grp", "brick", None),
            P("grp", "brick"),
            P(),
            P(),
            P(),
            P(),
        ),
        out_specs=(
            P("brick", None, "grp"),
            P("brick", None, "grp"),
            P("brick", None, "grp"),
            P("grp", "brick", None, None),
        ),
        check_vma=False,
    )
```

```python
import functools

import jax
import jax.numpy as jnp
from jax import lax
from jax.experimental import pallas as pl
from jax.experimental.pallas import tpu as pltpu
from jax.sharding import PartitionSpec as P

NEWTON = 2
SWEEPS = 8
courant = 0.8
f32 = jnp.float32
bf16 = jnp.bfloat16
BLOCK = 256
MESH = pl.DeviceIdType.MESH


def split(values):
    high = values.astype(bf16)
    low = (values - high.astype(f32)).astype(bf16)
    return high, low


def dot(a, b, dims=((1,), (0,))):
    return lax.dot_general(a, b, (dims, ((), ())), preferred_element_type=f32)


def five_point(lower2, lower1, upper1, upper2):
    return 8.0 * (upper1 - lower1) - (upper2 - lower2)


def y_part(g):
    n = g.shape[0]
    return five_point(
        pltpu.roll(g, 2, 0), pltpu.roll(g, 1, 0), pltpu.roll(g, n - 1, 0), pltpu.roll(g, n - 2, 0)
    )


def z_part(h, other):
    n = h.shape[1]
    lane = lax.broadcasted_iota(jnp.int32, h.shape, 1)
    return five_point(
        pltpu.roll(jnp.where(lane >= n - 2, other, h), 2, 1),
        pltpu.roll(jnp.where(lane >= n - 1, other, h), 1, 1),
        pltpu.roll(jnp.where(lane < 1, other, h), n - 1, 1),
        pltpu.roll(jnp.where(lane < 2, other, h), n - 2, 1),
    )


def kernel(
    axis_sizes,
    count_ref,
    rho_ref,
    eps_ref,
    lam_ref,
    vel_ref,
    rows_ref,
    mass_ref,
    cell_ref,
    weak_ref,
    capture_ref,
    binding_ref,
    charge_ref,
    density_out,
    energy_out,
    lepton_out,
    abundance_out,
    xs,
    zs,
    low_in,
    high_in,
    z_in,
    mid,
    weights,
    onehot,
    rate_weak,
    rate_capture,
    start_rows,
    alpha_capture,
    scaled_capture,
    target,
    update,
    deposit,
    send_sem,
    recv_sem,
):
    n_grp, n_brick = axis_sizes
    g = lax.axis_index("grp")
    b = lax.axis_index("brick")
    right = (g, lax.rem(b + 1, n_brick))
    left = (g, lax.rem(b + n_brick - 1, n_brick))
    partner = (lax.rem(g + 1, n_grp), b)
    fields = (rho_ref, eps_ref, lam_ref)
    outs = (density_out, energy_out, lepton_out)
    cx, cy, cz = rho_ref.shape
    capacity, species = rows_ref.shape

    barrier = pltpu.get_barrier_semaphore()
    for neighbour in (left, right, partner):
        pl.semaphore_signal(barrier, inc=1, device_id=neighbour, device_id_type=MESH)

    for f in range(3):
        for p in range(cx):
            xs[0, f, p] = vel_ref[0, p] * fields[f][p]
            zs[0, f, p] = vel_ref[2, p] * fields[f][p]

    pl.semaphore_wait(barrier, 3)

    def copies(stage, f):
        made = []
        for k, (src, dst, device) in enumerate(
            (
                (xs.at[stage, f, pl.ds(0, 2)], high_in.at[stage, f], left),
                (xs.at[stage, f, pl.ds(cx - 2, 2)], low_in.at[stage, f], right),
                (zs.at[stage, f], z_in.at[stage, f], partner),
            )
        ):
            made.append(
                pltpu.make_async_remote_copy(
                    src_ref=src,
                    dst_ref=dst,
                    send_sem=send_sem.at[stage, f, k],
                    recv_sem=recv_sem.at[stage, f, k],
                    device_id=device,
                    device_id_type=MESH,
                )
            )
        return made

    started = [[copies(stage, f) for f in range(3)] for stage in range(2)]
    for f in range(3):
        for copy in started[0][f]:
            copy.start()

    cells = cell_ref[...]
    cell_row = cells // cz
    cell_lane = cells - cell_row * cz
    row_ids = lax.broadcasted_iota(jnp.int32, (cx * cy, capacity), 0)
    onehot[...] = jnp.where(row_ids == cell_row, 1.0, 0.0).astype(bf16)
    lane_ids = lax.broadcasted_iota(jnp.int32, (cz, capacity), 0)
    lane_hit = lane_ids == cell_lane
    picked = []
    for f in range(3):
        high, low = split(fields[f][...].reshape(cx * cy, cz))
        found = dot(high, onehot[...], ((0,), (0,))) + dot(low, onehot[...], ((0,), (0,)))
        picked.append(jnp.sum(jnp.where(lane_hit, found, 0.0), axis=0, keepdims=True))
    rho, eps, lam = picked
    weak_row = 0.62 + 0.04 * rho + 0.05 * (lam / rho)
    capture_row = 0.3 * jax.nn.sigmoid(eps / rho)
    for k in range(capacity // 128):
        part = pl.ds(k * 128, 128)
        cols = slice(k * 128, k * 128 + 128)
        rate_weak[part, :] = jnp.broadcast_to(weak_row[:, cols], (128, 128)).T
        rate_capture[part, :] = jnp.broadcast_to(capture_row[:, cols], (128, 128)).T

    for k, ref in enumerate((weak_ref, capture_ref)):
        high, low = split(ref[...])
        cols = pl.ds(k * species, species)
        weights[0:species, cols] = high
        weights[species : 2 * species, cols] = high
        weights[2 * species : 3 * species, cols] = low

    count = count_ref[0, 0]
    for k in range(capacity // BLOCK):
        part = pl.ds(k * BLOCK, BLOCK)
        row = lax.broadcasted_iota(jnp.int32, (BLOCK, species), 0) + k * BLOCK
        first = jnp.where(row < count, rows_ref[part, :], 0.0)
        start_rows[part, :] = first
        abundance_out[part, :] = first

    def product(values):
        high, low = split(values)
        return dot(jnp.concatenate([high, low, high], axis=1), weights[...])

    def newton_start(turn):
        for k in range(capacity // BLOCK):
            part = pl.ds(k * BLOCK, BLOCK)
            now = abundance_out[part, :]
            made = product(now)
            capture = made[:, species:]
            scaled = rate_capture[part, :]
            alpha = scaled * now[:, 0:1]
            alpha_capture[part, :] = alpha
            scaled_capture[part, :] = scaled * capture
            aim = rate_weak[part, :] * made[:, :species] + alpha * capture
            if turn:
                aim = aim - (now - start_rows[part, :])
            target[part, :] = aim
            update[part, :] = aim

    def sweeps(number):
        def sweep(_, carry):
            for k in range(capacity // BLOCK):
                part = pl.ds(k * BLOCK, BLOCK)
                now = update[part, :]
                made = product(now)
                update[part, :] = target[part, :] + (
                    rate_weak[part, :] * made[:, :species]
                    + alpha_capture[part, :] * made[:, species:]
                    + scaled_capture[part, :] * now[:, 0:1]
                )
            return carry

        lax.fori_loop(0, number, sweep, 0)

    def newton_end():
        for k in range(capacity // BLOCK):
            part = pl.ds(k * BLOCK, BLOCK)
            abundance_out[part, :] = abundance_out[part, :] + update[part, :]

    def tendency(stage, f, field):
        results = []
        line = (
            [low_in[stage, f, 0], low_in[stage, f, 1]]
            + [xs[stage, f, p] for p in range(cx)]
            + [high_in[stage, f, 0], high_in[stage, f, 1]]
        )
        for p in range(cx):
            along_x = five_point(line[p], line[p + 1], line[p + 3], line[p + 4])
            along_y = y_part(vel_ref[1, p] * field[p])
            along_z = z_part(zs[stage, f, p], z_in[stage, f, p])
            results.append((along_x + along_y + along_z) * (-1.0 / 12.0))
        return results

    def half_step(f):
        for copy in started[0][f]:
            copy.wait_recv()
        slopes = tendency(0, f, [fields[f][p] for p in range(cx)])
        for p in range(cx):
            half = fields[f][p] + 0.5 * courant * slopes[p]
            mid[f, p] = half
            xs[1, f, p] = vel_ref[0, p] * half
            zs[1, f, p] = vel_ref[2, p] * half
        for copy in started[1][f]:
            copy.start()

    newton_start(0)
    sweeps(SWEEPS)
    newton_end()
    half_step(0)
    newton_start(1)
    sweeps(SWEEPS // 2)
    half_step(1)
    sweeps(SWEEPS - SWEEPS // 2)
    newton_end()
    half_step(2)

    change_high, change_low = split(abundance_out[...] - start_rows[...])
    table = jnp.concatenate(
        [binding_ref[...], charge_ref[...], jnp.zeros((6, species), f32)], axis=0
    )
    table_high, table_low = split(table)
    gains = (
        dot(table_high, change_high, ((1,), (1,)))
        + dot(table_high, change_low, ((1,), (1,)))
        + dot(table_low, change_high, ((1,), (1,)))
    ) * mass_ref[...]
    for k in range(2):
        placed = jnp.where(lane_hit, gains[k : k + 1, :], 0.0)
        high, low = split(placed)
        deposit[k] = (
            dot(onehot[...], high, ((1,), (1,))) + dot(onehot[...], low, ((1,), (1,)))
        ).reshape(cx, cy, cz)

    for f in range(3):
        for copy in started[1][f]:
            copy.wait_recv()
        slopes = tendency(1, f, [mid[f, p] for p in range(cx)])
        for p in range(cx):
            value = fields[f][p] + courant * slopes[p]
            if f:
                value = value + deposit[f - 1, p]
            outs[f][p] = value

    for stage in range(2):
        for f in range(3):
            for copy in started[stage][f]:
                copy.wait_send()


def settle(a_ref, b_ref, c_ref, d_ref, a_out, b_out, c_out, d_out, sem):
    pairs = ((d_ref, d_out), (a_ref, a_out), (b_ref, b_out), (c_ref, c_out))
    moves = [pltpu.make_async_copy(src, dst, sem.at[k]) for k, (src, dst) in enumerate(pairs)]
    for move in moves:
        move.start()
    for move in moves:
        move.wait()


def on_device(
    axis_sizes,
    density,
    energy_field,
    lepton_field,
    velocity,
    abundance,
    tracer_mass,
    tracer_cell,
    tracer_count,
    weak_rates,
    capture_rates,
    binding,
    charge_ratio,
):
    cx, cy, cz = density.shape
    capacity, species = abundance.shape[2:]
    vmem = pl.BlockSpec(memory_space=pltpu.VMEM)
    field = jax.ShapeDtypeStruct(density.shape, f32)
    rows = pltpu.VMEM((capacity, species), f32)
    advanced = pl.pallas_call(
        functools.partial(kernel, axis_sizes),
        out_shape=(pltpu.VMEM(density.shape, f32),) * 3 + (rows,),
        in_specs=[pl.BlockSpec(memory_space=pltpu.SMEM)] + [vmem] * 11,
        out_specs=(vmem,) * 4,
        scratch_shapes=[
            pltpu.VMEM((2, 3, cx, cy, cz), f32),
            pltpu.VMEM((2, 3, cx, cy, cz), f32),
            pltpu.VMEM((2, 3, 2, cy, cz), f32),
            pltpu.VMEM((2, 3, 2, cy, cz), f32),
            pltpu.VMEM((2, 3, cx, cy, cz), f32),
            pltpu.VMEM((3, cx, cy, cz), f32),
            pltpu.VMEM((3 * species, 2 * species), bf16),
            pltpu.VMEM((cx * cy, capacity), bf16),
            rows,
            rows,
            rows,
            rows,
            rows,
            rows,
            rows,
            pltpu.VMEM((2, cx, cy, cz), f32),
            pltpu.SemaphoreType.DMA((2, 3, 3)),
            pltpu.SemaphoreType.DMA((2, 3, 3)),
        ],
        compiler_params=pltpu.CompilerParams(collective_id=0, has_side_effects=True),
    )(
        tracer_count,
        density,
        energy_field,
        lepton_field,
        velocity,
        abundance.reshape(capacity, species),
        tracer_mass.reshape(1, capacity),
        tracer_cell.reshape(1, capacity),
        weak_rates,
        capture_rates,
        binding.reshape(1, species),
        charge_ratio.reshape(1, species),
    )
    whole = pl.BlockSpec(memory_space=pl.ANY)
    results = pl.pallas_call(
        settle,
        out_shape=(field, field, field, jax.ShapeDtypeStruct((capacity, species), f32)),
        in_specs=[whole] * 4,
        out_specs=(whole,) * 4,
        scratch_shapes=[pltpu.SemaphoreType.DMA((4,))],
    )(*[pltpu.with_memory_space_constraint(a, pltpu.VMEM) for a in advanced])
    return results[0], results[1], results[2], results[3][None, None]


def solution(mesh):
    sizes = (mesh.shape["grp"], mesh.shape["brick"])
    assert sizes[0] == 2
    return jax.shard_map(
        functools.partial(on_device, sizes),
        mesh=mesh,
        in_specs=(
            P("brick", None, "grp"),
            P("brick", None, "grp"),
            P("brick", None, "grp"),
            P(None, "brick", None, "grp"),
            P("grp", "brick", None, None),
            P("grp", "brick", None),
            P("grp", "brick", None),
            P("grp", "brick"),
            P(),
            P(),
            P(),
            P(),
        ),
        out_specs=(
            P("brick", None, "grp"),
            P("brick", None, "grp"),
            P("brick", None, "grp"),
            P("grp", "brick", None, None),
        ),
        check_vma=False,
    )
```
